32 devices in a mesh: grp: 2 (over y), smp: 4 (over z), st: 2 (over x), sub: 2 (over core).
Axes of the slice: x: 2, y: 2, z: 4, core: 2. Of those that a mesh axis runs over, the one named last changes fastest.
Arguments:
- energies: float32 [3072, 2048], P(('grp', 'smp'), ('st', 'sub')), parts along dimension 0, may hold values from -300 to 300
- counts: int32 [4096], P(('grp', 'st', 'sub')), parts along dimension 0, may hold values from 16 to 48
- labels: int32 [3072], P(('grp', 'smp')), parts along dimension 0, may hold values from 0 to 2047
Outputs:
- start_energy: float32 [4096], P(('grp', 'st', 'sub')), parts along dimension 0
- free_energy: float32 [4096], P(('grp', 'st', 'sub')), parts along dimension 0
- correlation: float32 [4096, 2048], P(('grp', 'smp'), ('st', 'sub')), parts along dimension 0
The draws below stay inside these ranges and needn't reach their ends.
There are 2 independent parts, one for each index of `grp`. The reference program is written for one: setup_inputs(seed, part) draws one part's arguments, and reference() takes and returns one part's arrays. A program takes and returns all parts, laid end to end along the dimension named above; each array names one. Nothing has to cross between parts.
All inputs are finite; a program needn't handle non-finite values.
Results may differ from the reference program's by a relative error of at most 0.0003.
Values sent between devices are 32-bit elements; how exact they have to be, the bound alone decides.
A program may use at most 64 MiB of HBM per device.

```python
import jax
import jax.numpy as jnp
from jax import lax

STATES = 2048
ITERS = 3
SAMPLES = 1536


def draw_energies(key, part):
    keys = jax.random.split(key, 6)
    position = jnp.arange(SAMPLES, dtype=jnp.float32)[:, None] / jnp.float32(SAMPLES - 1) - 0.5
    rough = 1.5 * jax.random.normal(keys[0], (SAMPLES, STATES), jnp.float32)
    col_shift = jax.random.uniform(keys[4], (1, STATES), jnp.float32, -2.0, 2.0)
    slope = jax.random.uniform(keys[5], (1, STATES), jnp.float32, -2.0, 2.0)
    return rough + col_shift + slope * position


def with_ends(entries, stream_key, smallest, high):
    dims = entries.shape
    index_at = [jax.random.randint(jax.random.fold_in(stream_key, axis), (), 0, dims[axis]) for axis in range(len(dims))]
    entries = entries.at[tuple(index_at)].set(smallest)
    longest = dims.index(max(dims))
    index_at[longest] = (index_at[longest] + 1) % dims[longest]
    return entries.at[tuple(index_at)].set(high)


def setup_inputs(seed: int = 0, part: int = 0) -> dict:
    seeds = jax.random.split(jax.random.key(seed), 4)
    own_keys = jax.random.split(jax.random.fold_in(seeds[3], part), 4)
    energies = draw_energies(jax.random.fold_in(jax.random.fold_in(seeds[3], part), 71), part)
    counts = with_ends(jax.random.randint(own_keys[1], (STATES,), 16, 49), jax.random.fold_in(own_keys[1], 1), 16, 48).astype(jnp.int32)
    labels = with_ends(jax.random.randint(own_keys[2], (SAMPLES,), 0, STATES), jax.random.fold_in(own_keys[2], 1), 0, STATES - 1).astype(jnp.int32)
    return {"energies": energies, "counts": counts, "labels": labels}


def lse_axis(values, axis):
    largest = jnp.max(values, axis=axis, keepdims=True)
    summed = jnp.sum(jnp.exp(values - largest), axis=axis)
    return jnp.squeeze(largest, axis) + jnp.log(summed)


def reference(energies, counts, labels):
    log_counts = jnp.log(counts.astype(jnp.float32))
    state_ids = jnp.arange(STATES, dtype=jnp.int32)
    anchor_hit = labels[:, None] == state_ids[None, :]
    energy_sums = jnp.sum(jnp.where(anchor_hit, energies, jnp.float32(0.0)), axis=0)
    label_counts = jnp.sum(anchor_hit.astype(jnp.float32), axis=0)
    start_energy = energy_sums / jnp.maximum(label_counts, jnp.float32(1.0))
    free_energy = start_energy
    for iteration in range(ITERS):
        log_denom = lse_axis(log_counts[None, :] + free_energy[None, :] - energies, 1)
        free_energy = -lse_axis(-energies - log_denom[:, None], 0)
    log_denom = lse_axis(log_counts[None, :] + free_energy[None, :] - energies, 1)
    weights = jnp.exp(free_energy[None, :] - energies - log_denom[:, None])
    gram = jnp.dot(weights.T, weights, precision=lax.Precision.HIGHEST)
    correlation = jnp.float32(STATES) * counts.astype(jnp.float32)[None, :] * gram
    return start_energy, free_energy, correlation
```

```python
import functools

import jax
import jax.numpy as jnp
from jax import lax
from jax.experimental import pallas as pl
from jax.experimental.pallas import tpu as pltpu
from jax.sharding import PartitionSpec as P

ITERS = 3
LANES = 128
HAND, RELAY, LAND = 2, 2, 1
MESH = pl.DeviceIdType.MESH


def to_lanes(col):
    return jnp.transpose(jnp.broadcast_to(col, (col.shape[0], LANES)))[0:1, :]


def to_rows(row, width):
    tall = jnp.transpose(jnp.broadcast_to(row, (LANES, row.shape[1])))
    return jnp.concatenate([tall] * (width // LANES), axis=1)


def lse_of(parts):
    peak = functools.reduce(jnp.maximum, parts)
    return peak + jnp.log(sum(jnp.exp(part - peak) for part in parts))


def split(values):
    high = values.astype(jnp.bfloat16)
    return high, (values - high.astype(jnp.float32)).astype(jnp.bfloat16)


def pairs(left, right):
    return lax.dot_general(
        left, right, (((0,), (0,)), ((), ())), preferred_element_type=jnp.float32
    )


def kernel(
    n, n_st, n_sub, chunks, rows_out,
    e_hbm, counts_ref, labels_ref, start_ref, free_ref, gram_ref,
    eall, erow, acc, sbuf, zbuf, xbuf, fbuf, lbuf,
    load_sem, zs, zr, xs, xr, bs, br, rs, rr,
):
    samples, width = eall.shape[1], eall.shape[2]
    window = erow.shape[2]
    nq = n_st * n_sub
    p, st, sub = lax.axis_index("smp"), lax.axis_index("st"), lax.axis_index("sub")
    q = st * n_sub + sub
    piece = samples // chunks
    ticks = (n - 1) * chunks
    lags = HAND + RELAY + LAND

    first_row = p * rows_out
    owner = lax.div(first_row, width)
    owner_st, owner_sub = lax.div(owner, n_sub), lax.rem(owner, n_sub)
    in_block = lax.rem(first_row, width)
    lane0 = pl.multiple_of(lax.div(in_block, window) * window, LANES)
    is_owner = jnp.logical_and(st == owner_st, sub == owner_sub)
    is_relay = jnp.logical_and(st != owner_st, sub == owner_sub)
    is_end = sub != owner_sub

    load = pltpu.make_async_copy(e_hbm, eall.at[p], load_sem)
    load.start()
    barrier = pltpu.get_barrier_semaphore()
    for k in range(1, n):
        pl.semaphore_signal(
            barrier, inc=1, device_id={"smp": lax.rem(p + k, n)}, device_id_type=MESH
        )

    def plane(k):
        peer = lax.rem(q + k, nq)
        return {"st": lax.div(peer, n_sub), "sub": lax.rem(peer, n_sub)}

    for k in range(1, nq):
        pl.semaphore_signal(barrier, inc=1, device_id=plane(k), device_id_type=MESH)
    pl.semaphore_wait(barrier, n - 1 + nq - 1)
    load.wait()

    def remote(src, dst, send, recv, where):
        return pltpu.make_async_remote_copy(
            src_ref=src, dst_ref=dst, send_sem=send, recv_sem=recv,
            device_id=where, device_id_type=MESH,
        )

    def z_copy(buf, phase, k, slot):
        return remote(
            buf.at[p], buf.at[slot], zs.at[phase, k], zr.at[phase, k],
            {"smp": lax.rem(p + k, n)},
        )

    def z_send(buf, phase):
        for k in range(n - 1, 0, -1):
            z_copy(buf, phase, k, p).start()

    def z_recv(buf, phase):
        for k in range(1, n):
            z_copy(buf, phase, k, lax.rem(p + n - k, n)).wait_recv()

    def x_copy(buf, phase, k, slot):
        return remote(buf.at[q], buf.at[slot], xs.at[phase, k], xr.at[phase, k], plane(k))

    def x_send(buf, phase):
        for k in range(1, nq):
            x_copy(buf, phase, k, q).start()

    def x_recv(buf, phase):
        for k in range(1, nq):
            x_copy(buf, phase, k, lax.rem(q + nq - k, nq)).wait_recv()

    def rows_of(c):
        return pl.ds(pl.multiple_of(c * piece, 8), piece)

    def bulk(way, t, block):
        view = eall.at[block, rows_of(lax.rem(t, chunks))]
        return remote(
            view, view, bs.at[way, t], br.at[way, t], {"smp": p + 1 if way == 0 else p - 1}
        )

    def sends(t):
        hop = lax.div(t, chunks)
        return (
            (0, p - hop, jnp.logical_and(p < n - 1, hop <= p)),
            (1, p + hop, jnp.logical_and(p > 0, hop <= n - 1 - p)),
        )

    def arrivals(t):
        hop = lax.div(t, chunks)
        good = t >= 0
        return (
            (0, p - 1 - hop, jnp.logical_and(good, hop <= p - 1)),
            (1, p + 1 + hop, jnp.logical_and(good, hop <= n - 2 - p)),
        )

    def events(t):
        own = jnp.logical_and(t >= 0, t < chunks)
        return ((None, p, own),) + arrivals(t)

    def row_local(block, c):
        src = eall.at[block, rows_of(c)]
        if window != width:
            src = eall.at[block, rows_of(c), pl.ds(lane0, window)]
        return pltpu.make_async_copy(src, erow.at[block, rows_of(c)], rr.at[block, c])

    def row_first(block, c, peer):
        src = eall.at[block, rows_of(c)]
        if window != width:
            src = eall.at[block, rows_of(c), pl.ds(lane0, window)]
        where = (
            {"st": lax.rem(st + peer, n_st)}
            if peer < n_st
            else {"sub": lax.rem(sub + peer - n_st + 1, n_sub)}
        )
        return remote(
            src, erow.at[block, rows_of(c)], rs.at[peer - 1, block, c], rr.at[block, c], where
        )

    def row_again(block, c, peer):
        view = erow.at[block, rows_of(c)]
        return remote(
            view, view, rs.at[peer - 1, block, c], rr.at[block, c],
            {"sub": lax.rem(sub + peer - n_st + 1, n_sub)},
        )

    first_peers = range(1, n_st + n_sub - 1)
    again_peers = range(n_st, n_st + n_sub - 1)

    def tick(t):
        t = jnp.int32(t)
        for way, block, good in sends(t):
            @pl.when(jnp.logical_and(good, t < ticks))
            def _():
                bulk(way, t, block).start()

        u = t - HAND
        c = lax.rem(u + chunks, chunks)
        for way, block, good in events(u):
            if way is not None:
                @pl.when(good)
                def _():
                    bulk(way, u, block).wait_recv()

            @pl.when(jnp.logical_and(good, is_owner))
            def _():
                for peer in first_peers:
                    row_first(block, c, peer).start()
                row_local(block, c).start()

        u2 = u - RELAY
        c2 = lax.rem(u2 + 2 * chunks, chunks)
        for way, block, good in events(u2):
            @pl.when(jnp.logical_and(good, is_owner))
            def _():
                row_local(block, c2).wait()

            @pl.when(jnp.logical_and(good, is_relay))
            def _():
                row_again(block, c2, again_peers[0] if again_peers else 1).wait_recv()
                for peer in again_peers:
                    row_again(block, c2, peer).start()

        u3 = u2 - LAND
        c3 = lax.rem(u3 + 6 * chunks, chunks)
        for way, block, good in events(u3):
            @pl.when(jnp.logical_and(good, is_end))
            def _():
                row_again(block, c3, n_st).wait_recv()

    plan = iter(range(10**6))

    energies = eall.at[p]
    label_rows = to_rows(labels_ref[...].astype(jnp.float32), width)
    state_ids = lax.broadcasted_iota(jnp.int32, (samples, width), 1) + q * width
    hit = label_rows == state_ids.astype(jnp.float32)
    sbuf[p, 0:1, :] = jnp.sum(jnp.where(hit, energies[...], jnp.float32(0.0)), axis=0, keepdims=True)
    sbuf[p, 1:2, :] = jnp.sum(hit.astype(jnp.float32), axis=0, keepdims=True)
    z_send(sbuf, 0)
    tick(next(plan))
    tick(next(plan))
    log_counts = jnp.log(counts_ref[...].astype(jnp.float32))
    z_recv(sbuf, 0)
    total = sum(sbuf[j] for j in range(n))
    start = total[0:1, :] / jnp.maximum(total[1:2, :], jnp.float32(1.0))
    start_ref[...] = start

    def row_lse(free, phase):
        scores = (log_counts + free) - energies[...]
        peak = jnp.max(scores, axis=1, keepdims=True)
        local = peak + jnp.log(jnp.sum(jnp.exp(scores - peak), axis=1, keepdims=True))
        here = xbuf.at[phase]
        here[q] = to_lanes(local)
        x_send(here, phase)
        tick(next(plan))
        x_recv(here, phase)
        return lse_of([here[j] for j in range(nq)])

    free = start
    for step in range(ITERS):
        denom = row_lse(free, step)
        scores = -energies[...] - to_rows(denom, width)
        peak = jnp.max(scores, axis=0, keepdims=True)
        local = peak + jnp.log(jnp.sum(jnp.exp(scores - peak), axis=0, keepdims=True))
        here = zbuf.at[step]
        here[p] = local
        z_send(here, step + 1)
        tick(next(plan))
        z_recv(here, step + 1)
        free = -lse_of([here[j] for j in range(n)])
    free_ref[...] = free
    fbuf[q] = free
    x_send(fbuf, ITERS + 1)
    denom = row_lse(free, ITERS)
    lbuf[p] = denom
    z_send(lbuf, ITERS + 1)
    tick(next(plan))
    acc[...] = jnp.zeros_like(acc)
    x_recv(fbuf, ITERS + 1)
    z_recv(lbuf, ITERS + 1)

    def add_block(block):
        denom_rows = to_rows(lbuf[block], LANES)
        row_free = fbuf[owner] if window == width else fbuf[owner, :, pl.ds(lane0, window)]

        def weights(free_row, view):
            wide = jnp.concatenate([denom_rows] * (view.shape[1] // LANES), axis=1)
            return split(
                jnp.exp(free_row - view[...] - wide)
            )

        col_high, col_low = weights(free_ref[...], eall.at[block])
        row_high, row_low = weights(row_free, erow.at[block])
        acc[...] += pairs(row_high, col_high) + (
            pairs(row_high, col_low) + pairs(row_low, col_high)
        )

    def add_hop(hop, carry):
        def side(s, inner):
            block = jnp.where(s == 0, p, jnp.where(s == 1, p - 1 - hop, p + 1 + hop))
            good = jnp.where(
                s == 0, hop == 0, jnp.where(s == 1, hop <= p - 1, hop <= n - 2 - p)
            )

            @pl.when(good)
            def _():
                add_block(block)

            return inner

        lax.fori_loop(0, 3, side, 0)
        return carry

    def tail(t, carry):
        tick(t)
        done = t - lags + 1

        @pl.when(jnp.logical_and(done > 0, lax.rem(done, chunks) == 0))
        def _():
            add_hop(lax.div(done, chunks) - 1, 0)

        return carry

    first = next(plan)
    ready = min(max(0, (first - lags) // chunks), n - 1)
    if ready:
        lax.fori_loop(0, ready, add_hop, 0)
    lax.fori_loop(first, ticks + lags, tail, 0)

    if window == rows_out:
        gram_ref[...] = acc[...]
    else:
        inner_row = pl.multiple_of(in_block - lane0, 8)
        gram_ref[...] = acc[pl.ds(inner_row, rows_out), :]

    for k in range(1, n):
        z_copy(sbuf, 0, k, p).wait_send()
        for step in range(ITERS):
            z_copy(zbuf.at[step], step + 1, k, p).wait_send()
        z_copy(lbuf, ITERS + 1, k, p).wait_send()
    for k in range(1, nq):
        for phase in range(ITERS + 1):
            x_copy(xbuf.at[phase], phase, k, q).wait_send()
        x_copy(fbuf, ITERS + 1, k, q).wait_send()

    def drain_bulk(t, carry):
        for way, block, good in sends(t):
            @pl.when(good)
            def _():
                bulk(way, t, block).wait_send()
        return carry

    lax.fori_loop(0, ticks, drain_bulk, 0)

    def drain_rows(i, carry):
        block, c = lax.div(i, chunks), lax.rem(i, chunks)

        @pl.when(is_owner)
        def _():
            for peer in first_peers:
                row_first(block, c, peer).wait_send()

        @pl.when(is_relay)
        def _():
            for peer in again_peers:
                row_again(block, c, peer).wait_send()

        return carry

    lax.fori_loop(0, n * chunks, drain_rows, 0)


def per_device(sizes, energies, counts, labels):
    n, n_st, n_sub = sizes
    nq = n_st * n_sub
    samples, width = energies.shape
    rows_out = width * nq // n
    window = max(rows_out, LANES)
    chunks = 6 if n <= 8 else 1
    f32 = jnp.float32
    vmem = pl.BlockSpec(memory_space=pltpu.VMEM)
    dma = pltpu.SemaphoreType.DMA
    start, free, gram = pl.pallas_call(
        functools.partial(kernel, n, n_st, n_sub, chunks, rows_out),
        out_shape=(
            jax.ShapeDtypeStruct((1, width), f32),
            jax.ShapeDtypeStruct((1, width), f32),
            jax.ShapeDtypeStruct((rows_out, width), f32),
        ),
        in_specs=[pl.BlockSpec(memory_space=pl.ANY), vmem, vmem],
        out_specs=(vmem, vmem, vmem),
        scratch_shapes=[
            pltpu.VMEM((n, samples, width), f32),
            pltpu.VMEM((n, samples, window), f32),
            pltpu.VMEM((window, width), f32),
            pltpu.VMEM((n, 2, width), f32),
            pltpu.VMEM((ITERS, n, 1, width), f32),
            pltpu.VMEM((ITERS + 1, nq, 1, samples), f32),
            pltpu.VMEM((nq, 1, width), f32),
            pltpu.VMEM((n, 1, samples), f32),
            dma,
            dma((ITERS + 2, n)),
            dma((ITERS + 2, n)),
            dma((ITERS + 2, nq)),
            dma((ITERS + 2, nq)),
            dma((2, (n - 1) * chunks)),
            dma((2, (n - 1) * chunks)),
            dma((n_st + n_sub - 2, n, chunks)),
            dma((n, chunks)),
        ],
        compiler_params=pltpu.CompilerParams(
            collective_id=0, has_side_effects=True, vmem_limit_bytes=56 * 1024 * 1024
        ),
    )(energies, counts.reshape(1, width), labels.reshape(1, samples))
    scale = jnp.float32(width * nq) * counts.astype(f32)
    return start.reshape(width), free.reshape(width), scale[None, :] * gram


def solution(mesh):
    sizes = (mesh.shape["smp"], mesh.shape["st"], mesh.shape["sub"])
    return jax.shard_map(
        functools.partial(per_device, sizes),
        mesh=mesh,
        in_specs=(P(("grp", "smp"), ("st", "sub")), P(("grp", "st", "sub")), P(("grp", "smp"))),
        out_specs=(
            P(("grp", "st", "sub")),
            P(("grp", "st", "sub")),
            P(("grp", "smp"), ("st", "sub")),
        ),
        check_vma=False,
    )
```

```python
import functools

import jax
import jax.numpy as jnp
from jax import lax
from jax.experimental import pallas as pl
from jax.experimental.pallas import tpu as pltpu
from jax.sharding import PartitionSpec as P

ITERS = 3
LANES = 128
HAND, RELAY, LAND = 4, 4, 1
CHUNKS, HEAD, ZT, XT = 8, 3, 3, 1
MESH = pl.DeviceIdType.MESH


def to_lanes(col):
    return jnp.transpose(jnp.broadcast_to(col, (col.shape[0], LANES)))[0:1, :]


def to_rows(row, width):
    tall = jnp.transpose(jnp.broadcast_to(row, (LANES, row.shape[1])))
    return jnp.concatenate([tall] * (width // LANES), axis=1)


def lse_of(parts):
    peak = functools.reduce(jnp.maximum, parts)
    return peak + jnp.log(sum(jnp.exp(part - peak) for part in parts))


def split(values):
    high = values.astype(jnp.bfloat16)
    return high, (values - high.astype(jnp.float32)).astype(jnp.bfloat16)


def pairs(left, right):
    return lax.dot_general(
        left, right, (((0,), (0,)), ((), ())), preferred_element_type=jnp.float32
    )


def kernel(
    n, n_st, n_sub, chunks, rows_out,
    e_hbm, counts_ref, labels_ref, start_ref, free_ref, gram_ref,
    eall, erow, acc, sbuf, zbuf, xbuf, fbuf, lbuf,
    load_sem, zs, zr, xs, xr, bs, br, rs, rr,
):
    samples, width = eall.shape[1], eall.shape[2]
    window = erow.shape[2]
    nq = n_st * n_sub
    p, st, sub = lax.axis_index("smp"), lax.axis_index("st"), lax.axis_index("sub")
    q = st * n_sub + sub
    piece = samples // chunks
    ticks = (n - 1) * chunks
    lags = HAND + RELAY + LAND

    first_row = p * rows_out
    owner = lax.div(first_row, width)
    owner_st, owner_sub = lax.div(owner, n_sub), lax.rem(owner, n_sub)
    in_block = lax.rem(first_row, width)
    lane0 = pl.multiple_of(lax.div(in_block, window) * window, LANES)
    is_owner = jnp.logical_and(st == owner_st, sub == owner_sub)
    is_relay = jnp.logical_and(st != owner_st, sub == owner_sub)
    is_end = sub != owner_sub

    load = pltpu.make_async_copy(e_hbm, eall.at[p], load_sem)
    load.start()
    barrier = pltpu.get_barrier_semaphore()
    for k in range(1, n):
        pl.semaphore_signal(
            barrier, inc=1, device_id={"smp": lax.rem(p + k, n)}, device_id_type=MESH
        )

    def plane(k):
        peer = lax.rem(q + k, nq)
        return {"st": lax.div(peer, n_sub), "sub": lax.rem(peer, n_sub)}

    for k in range(1, nq):
        pl.semaphore_signal(barrier, inc=1, device_id=plane(k), device_id_type=MESH)
    pl.semaphore_wait(barrier, n - 1 + nq - 1)
    load.wait()

    def remote(src, dst, send, recv, where):
        return pltpu.make_async_remote_copy(
            src_ref=src, dst_ref=dst, send_sem=send, recv_sem=recv,
            device_id=where, device_id_type=MESH,
        )

    def z_copy(buf, phase, k, slot):
        return remote(
            buf.at[p], buf.at[slot], zs.at[phase, k], zr.at[phase, k],
            {"smp": lax.rem(p + k, n)},
        )

    def z_send(buf, phase):
        for k in range(n - 1, 0, -1):
            z_copy(buf, phase, k, p).start()

    def z_recv(buf, phase):
        for k in range(1, n):
            z_copy(buf, phase, k, lax.rem(p + n - k, n)).wait_recv()

    def x_copy(buf, phase, k, slot):
        return remote(buf.at[q], buf.at[slot], xs.at[phase, k], xr.at[phase, k], plane(k))

    def x_send(buf, phase):
        for k in range(1, nq):
            x_copy(buf, phase, k, q).start()

    def x_recv(buf, phase):
        for k in range(1, nq):
            x_copy(buf, phase, k, lax.rem(q + nq - k, nq)).wait_recv()

    def rows_of(c):
        return pl.ds(pl.multiple_of(c * piece, 8), piece)

    def bulk(way, t, block):
        view = eall.at[block, rows_of(lax.rem(t, chunks))]
        return remote(
            view, view, bs.at[way, t], br.at[way, t], {"smp": p + 1 if way == 0 else p - 1}
        )

    def sends(t):
        hop = lax.div(t, chunks)
        return (
            (0, p - hop, jnp.logical_and(p < n - 1, hop <= p)),
            (1, p + hop, jnp.logical_and(p > 0, hop <= n - 1 - p)),
        )

    def arrivals(t):
        hop = lax.div(t, chunks)
        good = t >= 0
        return (
            (0, p - 1 - hop, jnp.logical_and(good, hop <= p - 1)),
            (1, p + 1 + hop, jnp.logical_and(good, hop <= n - 2 - p)),
        )

    def events(t):
        own = jnp.logical_and(t >= 0, t < chunks)
        return ((None, p, own),) + arrivals(t)

    def row_local(block, c):
        src = eall.at[block, rows_of(c)]
        if window != width:
            src = eall.at[block, rows_of(c), pl.ds(lane0, window)]
        return pltpu.make_async_copy(src, erow.at[block, rows_of(c)], rr.at[block, c])

    def row_first(block, c, peer):
        src = eall.at[block, rows_of(c)]
        if window != width:
            src = eall.at[block, rows_of(c), pl.ds(lane0, window)]
        where = (
            {"st": lax.rem(st + peer, n_st)}
            if peer < n_st
            else {"sub": lax.rem(sub + peer - n_st + 1, n_sub)}
        )
        return remote(
            src, erow.at[block, rows_of(c)], rs.at[peer - 1, block, c], rr.at[block, c], where
        )

    def row_again(block, c, peer):
        view = erow.at[block, rows_of(c)]
        return remote(
            view, view, rs.at[peer - 1, block, c], rr.at[block, c],
            {"sub": lax.rem(sub + peer - n_st + 1, n_sub)},
        )

    first_peers = range(1, n_st + n_sub - 1)
    again_peers = range(n_st, n_st + n_sub - 1)

    def tick(t):
        t = jnp.int32(t)
        for way, block, good in sends(t):
            @pl.when(jnp.logical_and(good, t < ticks))
            def _():
                bulk(way, t, block).start()

        u = t - HAND
        c = lax.rem(u + chunks, chunks)
        for way, block, good in events(u):
            if way is not None:
                @pl.when(good)
                def _():
                    bulk(way, u, block).wait_recv()

            @pl.when(jnp.logical_and(good, is_owner))
            def _():
                for peer in first_peers:
                    row_first(block, c, peer).start()
                row_local(block, c).start()

        u2 = u - RELAY
        c2 = lax.rem(u2 + 2 * chunks, chunks)
        for way, block, good in events(u2):
            @pl.when(jnp.logical_and(good, is_owner))
            def _():
                row_local(block, c2).wait()

            @pl.when(jnp.logical_and(good, is_relay))
            def _():
                row_again(block, c2, again_peers[0] if again_peers else 1).wait_recv()
                for peer in again_peers:
                    row_again(block, c2, peer).start()

        u3 = u2 - LAND
        c3 = lax.rem(u3 + 6 * chunks, chunks)
        for way, block, good in events(u3):
            @pl.when(jnp.logical_and(good, is_end))
            def _():
                row_again(block, c3, n_st).wait_recv()

    plan = iter(range(10**6))

    def ticks_now(count):
        for _ in range(count):
            tick(next(plan))

    ticks_now(HEAD)

    energies = eall.at[p]
    label_rows = to_rows(labels_ref[...].astype(jnp.float32).reshape(1, samples), width)
    state_ids = lax.broadcasted_iota(jnp.int32, (samples, width), 1) + q * width
    hit = label_rows == state_ids.astype(jnp.float32)
    sbuf[p, 0:1, :] = jnp.sum(jnp.where(hit, energies[...], jnp.float32(0.0)), axis=0, keepdims=True)
    sbuf[p, 1:2, :] = jnp.sum(hit.astype(jnp.float32), axis=0, keepdims=True)
    z_send(sbuf, 0)
    ticks_now(ZT)
    log_counts = jnp.log(counts_ref[...].astype(jnp.float32))
    z_recv(sbuf, 0)
    total = sum(sbuf[j] for j in range(n))
    start = total[0:1, :] / jnp.maximum(total[1:2, :], jnp.float32(1.0))
    start_ref[...] = start

    def row_lse(free, phase):
        scores = (log_counts + free) - energies[...]
        peak = jnp.max(scores, axis=1, keepdims=True)
        local = peak + jnp.log(jnp.sum(jnp.exp(scores - peak), axis=1, keepdims=True))
        here = xbuf.at[phase]
        here[q] = to_lanes(local)
        x_send(here, phase)
        ticks_now(XT)
        x_recv(here, phase)
        return lse_of([here[j] for j in range(nq)])

    free = start
    for step in range(ITERS):
        denom = row_lse(free, step)
        scores = -energies[...] - to_rows(denom, width)
        peak = jnp.max(scores, axis=0, keepdims=True)
        local = peak + jnp.log(jnp.sum(jnp.exp(scores - peak), axis=0, keepdims=True))
        here = zbuf.at[step]
        here[p] = local
        z_send(here, step + 1)
        ticks_now(ZT)
        z_recv(here, step + 1)
        free = -lse_of([here[j] for j in range(n)])
    free_ref[...] = free
    fbuf[q] = free
    x_send(fbuf, ITERS + 1)
    denom = row_lse(free, ITERS)
    lbuf[p] = denom
    z_send(lbuf, ITERS + 1)
    ticks_now(ZT)
    acc[...] = jnp.zeros_like(acc)
    x_recv(fbuf, ITERS + 1)
    z_recv(lbuf, ITERS + 1)

    def add_block(block):
        denom_rows = to_rows(lbuf[block], LANES)
        row_free = fbuf[owner] if window == width else fbuf[owner, :, pl.ds(lane0, window)]

        def weights(free_row, view):
            wide = jnp.concatenate([denom_rows] * (view.shape[1] // LANES), axis=1)
            return split(
                jnp.exp(free_row - view[...] - wide)
            )

        col_high, col_low = weights(free_ref[...], eall.at[block])
        row_high, row_low = weights(row_free, erow.at[block])
        acc[...] += pairs(row_high, col_high) + (
            pairs(row_high, col_low) + pairs(row_low, col_high)
        )

    def add_hop(hop, carry):
        def side(s, inner):
            block = jnp.where(s == 0, p, jnp.where(s == 1, p - 1 - hop, p + 1 + hop))
            good = jnp.where(
                s == 0, hop == 0, jnp.where(s == 1, hop <= p - 1, hop <= n - 2 - p)
            )

            @pl.when(good)
            def _():
                add_block(block)

            return inner

        lax.fori_loop(0, 3, side, 0)
        return carry

    def tail(t, carry):
        tick(t)
        done = t - lags + 1

        @pl.when(jnp.logical_and(done > 0, lax.rem(done, chunks) == 0))
        def _():
            add_hop(lax.div(done, chunks) - 1, 0)

        return carry

    first = next(plan)
    ready = min(max(0, (first - lags) // chunks), n - 1)
    if ready:
        lax.fori_loop(0, ready, add_hop, 0)
    lax.fori_loop(first, ticks + lags, tail, 0)

    if window == rows_out:
        gram_ref[...] = acc[...]
    else:
        inner_row = pl.multiple_of(in_block - lane0, 8)
        gram_ref[...] = acc[pl.ds(inner_row, rows_out), :]

    for k in range(1, n):
        z_copy(sbuf, 0, k, p).wait_send()
        for step in range(ITERS):
            z_copy(zbuf.at[step], step + 1, k, p).wait_send()
        z_copy(lbuf, ITERS + 1, k, p).wait_send()
    for k in range(1, nq):
        for phase in range(ITERS + 1):
            x_copy(xbuf.at[phase], phase, k, q).wait_send()
        x_copy(fbuf, ITERS + 1, k, q).wait_send()

    def drain_bulk(t, carry):
        for way, block, good in sends(t):
            @pl.when(good)
            def _():
                bulk(way, t, block).wait_send()
        return carry

    lax.fori_loop(0, ticks, drain_bulk, 0)

    def drain_rows(i, carry):
        block, c = lax.div(i, chunks), lax.rem(i, chunks)

        @pl.when(is_owner)
        def _():
            for peer in first_peers:
                row_first(block, c, peer).wait_send()

        @pl.when(is_relay)
        def _():
            for peer in again_peers:
                row_again(block, c, peer).wait_send()

        return carry

    lax.fori_loop(0, n * chunks, drain_rows, 0)


def per_device(sizes, energies, counts, labels):
    n, n_st, n_sub = sizes
    nq = n_st * n_sub
    samples, width = energies.shape
    rows_out = width * nq // n
    window = max(rows_out, LANES)
    chunks = CHUNKS
    f32 = jnp.float32
    vmem = pl.BlockSpec(memory_space=pltpu.VMEM)
    dma = pltpu.SemaphoreType.DMA
    start, free, gram = pl.pallas_call(
        functools.partial(kernel, n, n_st, n_sub, chunks, rows_out),
        out_shape=(
            jax.ShapeDtypeStruct((1, width), f32),
            jax.ShapeDtypeStruct((1, width), f32),
            jax.ShapeDtypeStruct((rows_out, width), f32),
        ),
        in_specs=[pl.BlockSpec(memory_space=pl.ANY), vmem, vmem],
        out_specs=(vmem, vmem, vmem),
        scratch_shapes=[
            pltpu.VMEM((n, samples, width), f32),
            pltpu.VMEM((n, samples, window), f32),
            pltpu.VMEM((window, width), f32),
            pltpu.VMEM((n, 2, width), f32),
            pltpu.VMEM((ITERS, n, 1, width), f32),
            pltpu.VMEM((ITERS + 1, nq, 1, samples), f32),
            pltpu.VMEM((nq, 1, width), f32),
            pltpu.VMEM((n, 1, samples), f32),
            dma,
            dma((ITERS + 2, n)),
            dma((ITERS + 2, n)),
            dma((ITERS + 2, nq)),
            dma((ITERS + 2, nq)),
            dma((2, (n - 1) * chunks)),
            dma((2, (n - 1) * chunks)),
            dma((n_st + n_sub - 2, n, chunks)),
            dma((n, chunks)),
        ],
        compiler_params=pltpu.CompilerParams(
            collective_id=0, has_side_effects=True, vmem_limit_bytes=56 * 1024 * 1024
        ),
    )(energies, counts.reshape(1, width), labels)
    scale = jnp.float32(width * nq) * counts.astype(f32)
    return start.reshape(width), free.reshape(width), scale[None, :] * gram


def solution(mesh):
    sizes = (mesh.shape["smp"], mesh.shape["st"], mesh.shape["sub"])
    return jax.shard_map(
        functools.partial(per_device, sizes),
        mesh=mesh,
        in_specs=(P(("grp", "smp"), ("st", "sub")), P(("grp", "st", "sub")), P(("grp", "smp"))),
        out_specs=(
            P(("grp", "st", "sub")),
            P(("grp", "st", "sub")),
            P(("grp", "smp"), ("st", "sub")),
        ),
        check_vma=False,
    )
```

```python
import functools

import jax
import jax.numpy as jnp
from jax import lax
from jax.experimental import pallas as pl
from jax.experimental.pallas import tpu as pltpu
from jax.sharding import PartitionSpec as P

ITERS = 3
LANES = 128
HAND, RELAY, LAND = 4, 4, 1
CHUNKS, HEAD, ZT, XT = 8, 4, 3, 1
MESH = pl.DeviceIdType.MESH


def to_lanes(col):
    return jnp.transpose(jnp.broadcast_to(col, (col.shape[0], LANES)))[0:1, :]


def to_rows(row, width):
    tall = jnp.transpose(jnp.broadcast_to(row, (LANES, row.shape[1])))
    return jnp.concatenate([tall] * (width // LANES), axis=1)


def lse_of(parts):
    peak = functools.reduce(jnp.maximum, parts)
    return peak + jnp.log(sum(jnp.exp(part - peak) for part in parts))


def split(values):
    high = values.astype(jnp.bfloat16)
    return high, (values - high.astype(jnp.float32)).astype(jnp.bfloat16)


def pairs(left, right):
    return lax.dot_general(
        left, right, (((0,), (0,)), ((), ())), preferred_element_type=jnp.float32
    )


def kernel(
    n, n_st, n_sub, chunks, rows_out,
    e_hbm, counts_ref, labels_ref, start_ref, free_ref, gram_ref,
    eall, erow, acc, sbuf, zbuf, xbuf, fbuf, lbuf,
    load_sem, zs, zr, xs, xr, bs, br, rs, rr,
):
    samples, width = eall.shape[1], eall.shape[2]
    window = erow.shape[2]
    nq = n_st * n_sub
    p, st, sub = lax.axis_index("smp"), lax.axis_index("st"), lax.axis_index("sub")
    q = st * n_sub + sub
    piece = samples // chunks
    ticks = (n - 1) * chunks
    lags = HAND + RELAY + LAND

    first_row = p * rows_out
    owner = lax.div(first_row, width)
    owner_st, owner_sub = lax.div(owner, n_sub), lax.rem(owner, n_sub)
    in_block = lax.rem(first_row, width)
    lane0 = pl.multiple_of(lax.div(in_block, window) * window, LANES)
    is_owner = jnp.logical_and(st == owner_st, sub == owner_sub)
    is_relay = jnp.logical_and(st != owner_st, sub == owner_sub)
    is_end = sub != owner_sub

    load = pltpu.make_async_copy(e_hbm, eall.at[p], load_sem)
    load.start()
    barrier = pltpu.get_barrier_semaphore()
    for k in range(1, n):
        pl.semaphore_signal(
            barrier, inc=1, device_id={"smp": lax.rem(p + k, n)}, device_id_type=MESH
        )

    def plane(k):
        peer = lax.rem(q + k, nq)
        return {"st": lax.div(peer, n_sub), "sub": lax.rem(peer, n_sub)}

    for k in range(1, nq):
        pl.semaphore_signal(barrier, inc=1, device_id=plane(k), device_id_type=MESH)
    pl.semaphore_wait(barrier, n - 1 + nq - 1)
    load.wait()

    def remote(src, dst, send, recv, where):
        return pltpu.make_async_remote_copy(
            src_ref=src, dst_ref=dst, send_sem=send, recv_sem=recv,
            device_id=where, device_id_type=MESH,
        )

    def z_copy(buf, phase, k, slot):
        return remote(
            buf.at[p], buf.at[slot], zs.at[phase, k], zr.at[phase, k],
            {"smp": lax.rem(p + k, n)},
        )

    def z_send(buf, phase):
        for k in range(n - 1, 0, -1):
            z_copy(buf, phase, k, p).start()

    def z_recv(buf, phase):
        for k in range(1, n):
            z_copy(buf, phase, k, lax.rem(p + n - k, n)).wait_recv()

    def x_copy(buf, phase, k, slot):
        return remote(buf.at[q], buf.at[slot], xs.at[phase, k], xr.at[phase, k], plane(k))

    def x_send(buf, phase):
        for k in range(1, nq):
            x_copy(buf, phase, k, q).start()

    def x_recv(buf, phase):
        for k in range(1, nq):
            x_copy(buf, phase, k, lax.rem(q + nq - k, nq)).wait_recv()

    def rows_of(c):
        return pl.ds(pl.multiple_of(c * piece, 8), piece)

    def bulk(way, t, block):
        view = eall.at[block, rows_of(lax.rem(t, chunks))]
        return remote(
            view, view, bs.at[way, t], br.at[way, t], {"smp": p + 1 if way == 0 else p - 1}
        )

    def sends(t):
        hop = lax.div(t, chunks)
        return (
            (0, p - hop, jnp.logical_and(p < n - 1, hop <= p)),
            (1, p + hop, jnp.logical_and(p > 0, hop <= n - 1 - p)),
        )

    def arrivals(t):
        hop = lax.div(t, chunks)
        good = t >= 0
        return (
            (0, p - 1 - hop, jnp.logical_and(good, hop <= p - 1)),
            (1, p + 1 + hop, jnp.logical_and(good, hop <= n - 2 - p)),
        )

    def events(t):
        own = jnp.logical_and(t >= 0, t < chunks)
        return ((None, p, own),) + arrivals(t)

    def row_local(block, c):
        src = eall.at[block, rows_of(c)]
        if window != width:
            src = eall.at[block, rows_of(c), pl.ds(lane0, window)]
        return pltpu.make_async_copy(src, erow.at[block, rows_of(c)], rr.at[block, c])

    def row_first(block, c, peer):
        src = eall.at[block, rows_of(c)]
        if window != width:
            src = eall.at[block, rows_of(c), pl.ds(lane0, window)]
        where = (
            {"st": lax.rem(st + peer, n_st)}
            if peer < n_st
            else {"sub": lax.rem(sub + peer - n_st + 1, n_sub)}
        )
        return remote(
            src, erow.at[block, rows_of(c)], rs.at[peer - 1, block, c], rr.at[block, c], where
        )

    def row_again(block, c, peer):
        view = erow.at[block, rows_of(c)]
        return remote(
            view, view, rs.at[peer - 1, block, c], rr.at[block, c],
            {"sub": lax.rem(sub + peer - n_st + 1, n_sub)},
        )

    first_peers = range(1, n_st + n_sub - 1)
    again_peers = range(n_st, n_st + n_sub - 1)

    def tick(t):
        t = jnp.int32(t)
        for way, block, good in sends(t):
            @pl.when(jnp.logical_and(good, t < ticks))
            def _():
                bulk(way, t, block).start()

        u = t - HAND
        c = lax.rem(u + chunks, chunks)
        for way, block, good in events(u):
            if way is not None:
                @pl.when(good)
                def _():
                    bulk(way, u, block).wait_recv()

            @pl.when(jnp.logical_and(good, is_owner))
            def _():
                for peer in first_peers:
                    row_first(block, c, peer).start()
                if window != width:
                    row_local(block, c).start()

        u2 = u - RELAY
        c2 = lax.rem(u2 + 2 * chunks, chunks)
        for way, block, good in events(u2):
            if window != width:
                @pl.when(jnp.logical_and(good, is_owner))
                def _():
                    row_local(block, c2).wait()

            @pl.when(jnp.logical_and(good, is_relay))
            def _():
                row_again(block, c2, again_peers[0] if again_peers else 1).wait_recv()
                for peer in again_peers:
                    row_again(block, c2, peer).start()

        u3 = u2 - LAND
        c3 = lax.rem(u3 + 6 * chunks, chunks)
        for way, block, good in events(u3):
            @pl.when(jnp.logical_and(good, is_end))
            def _():
                row_again(block, c3, n_st).wait_recv()

    plan = iter(range(10**6))

    def ticks_now(count):
        for _ in range(count):
            tick(next(plan))

    ticks_now(HEAD)

    energies = eall.at[p]
    label_rows = to_rows(labels_ref[...].astype(jnp.float32).reshape(1, samples), width)
    state_ids = lax.broadcasted_iota(jnp.int32, (samples, width), 1) + q * width
    hit = label_rows == state_ids.astype(jnp.float32)
    sbuf[p, 0:1, :] = jnp.sum(jnp.where(hit, energies[...], jnp.float32(0.0)), axis=0, keepdims=True)
    sbuf[p, 1:2, :] = jnp.sum(hit.astype(jnp.float32), axis=0, keepdims=True)
    z_send(sbuf, 0)
    ticks_now(ZT)
    log_counts = jnp.log(counts_ref[...].astype(jnp.float32))
    z_recv(sbuf, 0)
    total = sum(sbuf[j] for j in range(n))
    start = total[0:1, :] / jnp.maximum(total[1:2, :], jnp.float32(1.0))
    start_ref[...] = start

    def row_lse(free, phase):
        scores = (log_counts + free) - energies[...]
        peak = jnp.max(scores, axis=1, keepdims=True)
        local = peak + jnp.log(jnp.sum(jnp.exp(scores - peak), axis=1, keepdims=True))
        here = xbuf.at[phase]
        here[q] = to_lanes(local)
        x_send(here, phase)
        ticks_now(XT)
        x_recv(here, phase)
        return lse_of([here[j] for j in range(nq)])

    free = start
    for step in range(ITERS):
        denom = row_lse(free, step)
        scores = -energies[...] - to_rows(denom, width)
        peak = jnp.max(scores, axis=0, keepdims=True)
        local = peak + jnp.log(jnp.sum(jnp.exp(scores - peak), axis=0, keepdims=True))
        here = zbuf.at[step]
        here[p] = local
        z_send(here, step + 1)
        ticks_now(ZT)
        z_recv(here, step + 1)
        free = -lse_of([here[j] for j in range(n)])
    free_ref[...] = free
    fbuf[q] = free
    x_send(fbuf, ITERS + 1)
    denom = row_lse(free, ITERS)
    lbuf[p] = denom
    z_send(lbuf, ITERS + 1)
    ticks_now(ZT)
    acc[...] = jnp.zeros_like(acc)
    x_recv(fbuf, ITERS + 1)
    z_recv(lbuf, ITERS + 1)

    def add_block(block, rows):
        denom_rows = to_rows(lbuf[block], LANES)
        row_free = fbuf[owner] if window == width else fbuf[owner, :, pl.ds(lane0, window)]

        def weights(free_row, view):
            wide = jnp.concatenate([denom_rows] * (view.shape[1] // LANES), axis=1)
            return split(
                jnp.exp(free_row - view[...] - wide)
            )

        col_high, col_low = weights(free_ref[...], eall.at[block])
        row_high, row_low = weights(row_free, rows.at[block])
        acc[...] += pairs(row_high, col_high) + (
            pairs(row_high, col_low) + pairs(row_low, col_high)
        )

    def add_hop(hop, carry):
        def side(s, inner):
            block = jnp.where(s == 0, p, jnp.where(s == 1, p - 1 - hop, p + 1 + hop))
            good = jnp.where(
                s == 0, hop == 0, jnp.where(s == 1, hop <= p - 1, hop <= n - 2 - p)
            )

            @pl.when(good)
            def _():
                if window != width:
                    add_block(block, erow)
                else:
                    @pl.when(is_owner)
                    def _():
                        add_block(block, eall)

                    @pl.when(jnp.logical_not(is_owner))
                    def _():
                        add_block(block, erow)

            return inner

        lax.fori_loop(0, 3, side, 0)
        return carry

    def tail(t, carry):
        tick(t)
        done = t - lags + 1

        @pl.when(jnp.logical_and(done > 0, lax.rem(done, chunks) == 0))
        def _():
            add_hop(lax.div(done, chunks) - 1, 0)

        return carry

    first = next(plan)
    ready = min(max(0, (first - lags) // chunks), n - 1)
    if ready:
        lax.fori_loop(0, ready, add_hop, 0)
    lax.fori_loop(first, ticks + lags, tail, 0)

    if window == rows_out:
        gram_ref[...] = acc[...]
    else:
        inner_row = pl.multiple_of(in_block - lane0, 8)
        gram_ref[...] = acc[pl.ds(inner_row, rows_out), :]

    for k in range(1, n):
        z_copy(sbuf, 0, k, p).wait_send()
        for step in range(ITERS):
            z_copy(zbuf.at[step], step + 1, k, p).wait_send()
        z_copy(lbuf, ITERS + 1, k, p).wait_send()
    for k in range(1, nq):
        for phase in range(ITERS + 1):
            x_copy(xbuf.at[phase], phase, k, q).wait_send()
        x_copy(fbuf, ITERS + 1, k, q).wait_send()

    def drain_bulk(t, carry):
        for way, block, good in sends(t):
            @pl.when(good)
            def _():
                bulk(way, t, block).wait_send()
        return carry

    lax.fori_loop(0, ticks, drain_bulk, 0)

    def drain_rows(i, carry):
        block, c = lax.div(i, chunks), lax.rem(i, chunks)

        @pl.when(is_owner)
        def _():
            for peer in first_peers:
                row_first(block, c, peer).wait_send()

        @pl.when(is_relay)
        def _():
            for peer in again_peers:
                row_again(block, c, peer).wait_send()

        return carry

    lax.fori_loop(0, n * chunks, drain_rows, 0)


def per_device(sizes, energies, counts, labels):
    n, n_st, n_sub = sizes
    nq = n_st * n_sub
    samples, width = energies.shape
    rows_out = width * nq // n
    window = max(rows_out, LANES)
    chunks = CHUNKS
    f32 = jnp.float32
    vmem = pl.BlockSpec(memory_space=pltpu.VMEM)
    dma = pltpu.SemaphoreType.DMA
    start, free, gram = pl.pallas_call(
        functools.partial(kernel, n, n_st, n_sub, chunks, rows_out),
        out_shape=(
            jax.ShapeDtypeStruct((1, width), f32),
            jax.ShapeDtypeStruct((1, width), f32),
            jax.ShapeDtypeStruct((rows_out, width), f32),
        ),
        in_specs=[pl.BlockSpec(memory_space=pl.ANY), vmem, vmem],
        out_specs=(vmem, vmem, vmem),
        scratch_shapes=[
            pltpu.VMEM((n, samples, width), f32),
            pltpu.VMEM((n, samples, window), f32),
            pltpu.VMEM((window, width), f32),
            pltpu.VMEM((n, 2, width), f32),
            pltpu.VMEM((ITERS, n, 1, width), f32),
            pltpu.VMEM((ITERS + 1, nq, 1, samples), f32),
            pltpu.VMEM((nq, 1, width), f32),
            pltpu.VMEM((n, 1, samples), f32),
            dma,
            dma((ITERS + 2, n)),
            dma((ITERS + 2, n)),
            dma((ITERS + 2, nq)),
            dma((ITERS + 2, nq)),
            dma((2, (n - 1) * chunks)),
            dma((2, (n - 1) * chunks)),
            dma((n_st + n_sub - 2, n, chunks)),
            dma((n, chunks)),
        ],
        compiler_params=pltpu.CompilerParams(
            collective_id=0, has_side_effects=True, vmem_limit_bytes=56 * 1024 * 1024
        ),
    )(energies, counts.reshape(1, width), labels)
    scale = jnp.float32(width * nq) * counts.astype(f32)
    return start.reshape(width), free.reshape(width), scale[None, :] * gram


def solution(mesh):
    sizes = (mesh.shape["smp"], mesh.shape["st"], mesh.shape["sub"])
    return jax.shard_map(
        functools.partial(per_device, sizes),
        mesh=mesh,
        in_specs=(P(("grp", "smp"), ("st", "sub")), P(("grp", "st", "sub")), P(("grp", "smp"))),
        out_specs=(
            P(("grp", "st", "sub")),
            P(("grp", "st", "sub")),
            P(("grp", "smp"), ("st", "sub")),
        ),
        check_vma=False,
    )
```
